32 devices in a mesh: ctx: 8 (over y, x, core), head: 4 (over z).
Axes of the slice: x: 2, y: 2, z: 4, core: 2. Of those that a mesh axis runs over, the one named last changes fastest.
Arguments:
- queries: bfloat16 [4096, 4096], P('ctx', 'head'), may hold values from -8 to 8
- keys: bfloat16 [4096, 1024], P('ctx', 'head'), may hold values from -8 to 8
- values: bfloat16 [4096, 1024], P('ctx', 'head'), may hold values from -6 to 6
- lengths: int32 [16], replicated, may hold values from 1 to 1024, 4096 in all
- out_weight: bfloat16 [4096, 4096], P(None, 'head'), may hold values from -0.09375 to 0.09375
Outputs:
- mixed: bfloat16 [4096, 4096], P('ctx', 'head')
The draws below stay inside these ranges and needn't reach their ends.
Inputs may be any that keep to these rules, and one draw needn't show every extreme that they name: `lengths`: each document holds at least one token and one holds exactly 1024; they sum to 4096.
All inputs are finite; a program needn't handle non-finite values.
Results may differ from the reference program's by a relative error of at most 0.0085.
Values may be sent and summed in bfloat16 or wider, within the bound.
No kernel may reach another device: no remote copies, remote signals or barrier semaphores. Data moves between devices by JAX's collectives and lax.ppermute only.
A program may use at most 64 MiB of HBM per device.

```python
import math
import jax
import jax.numpy as jnp
import numpy as np
from jax import lax

D = 4096
QUERY_HEADS = 32
KEY_VALUE_HEADS = 8
HEAD_SIZE = 128
TOK_DEV = 512
PACK_TOKENS = 4096
DOCS = 16
MOST = 1024


def starting_field_name(key, heads):
    return jnp.clip(jax.random.normal(key, (PACK_TOKENS, heads, HEAD_SIZE), jnp.float32), -6.0, 6.0)


def draw_queries(key, part):
    field_name = starting_field_name(jax.random.fold_in(key, 11), QUERY_HEADS)
    return field_name.reshape(PACK_TOKENS, QUERY_HEADS * HEAD_SIZE).astype(jnp.bfloat16)


def draw_keys(key, part):
    field_name = starting_field_name(jax.random.fold_in(key, 13), KEY_VALUE_HEADS)
    return field_name.reshape(PACK_TOKENS, KEY_VALUE_HEADS * HEAD_SIZE).astype(jnp.bfloat16)


def block_scale(rng, extent, split, low, top_value):
    def one(axis_at, shards_of):
        steps = jax.random.uniform(jax.random.fold_in(jax.random.fold_in(rng, 6), axis_at), (shards_of,), jnp.float32, low / len(split), top_value / len(split))
        return jnp.repeat(jnp.exp(steps), extent[axis_at] // shards_of).reshape((-1,) + (1,) * (len(extent) - axis_at - 1))

    level = one(*split[0])
    for cut in split[1:]:
        level = level * one(*cut)
    return level


def profile(number_of, total, limit, slope):
    loads = [(1 << 20) // math.isqrt(standing ** slope) + 1 for standing in range(2, number_of + 1)]
    surplus, given = total - limit - (number_of - 1), [1] * (number_of - 1)
    while surplus > 0:
        movable = [i for i in range(number_of - 1) if given[i] < limit]
        whole, remaining = sum([loads[i] for i in movable]), surplus
        for i in movable:
            extra = min(limit - given[i], max(1, remaining * loads[i] // whole), surplus)
            given[i] = given[i] + extra
            surplus = surplus - extra
    return np.array([limit] + given)


def ragged_sizes(own_key, amount, total, reach, skew):
    if amount == 2:
        one = jax.random.randint(own_key, (), max(1, total - reach), min(reach, total - 1) + 1)
        return jnp.stack([one, total - one])
    sizes = jnp.asarray(profile(amount, total, reach, skew), jnp.int32)
    couples = (amount - 1) // 2
    source_of, sink = sizes[1:1 + 2 * couples:2], sizes[2:2 + 2 * couples:2]
    margin = jnp.minimum(source_of - 1, reach - sink)
    passed = jax.random.randint(jax.random.fold_in(own_key, 1), (couples,), 0, 1 << 20) % (margin + 1)
    sizes = sizes.at[1:1 + 2 * couples:2].set(source_of - passed).at[2:2 + 2 * couples:2].set(sink + passed)
    return sizes[jax.random.permutation(jax.random.fold_in(own_key, 2), amount)]


def gaussian(stream_key, extent, width, limit, shards=(), kind=jnp.bfloat16):
    factor_of = block_scale(stream_key, extent, shards, -0.22, 0.18) if shards else 1.0
    entries = jax.random.normal(stream_key, extent, jnp.float32) * width * factor_of
    return jnp.minimum(jnp.maximum(entries, -limit), limit).astype(kind)


def setup_inputs(seed: int = 0) -> dict:
    splits = jax.random.split(jax.random.key(seed), 6)
    return {
        "queries": draw_queries(jax.random.fold_in(splits[5], 71), 0),
        "keys": draw_keys(jax.random.fold_in(splits[5], 71), 0),
        "values": gaussian(splits[2], (PACK_TOKENS, KEY_VALUE_HEADS * HEAD_SIZE), 1.0, 6.0, ((0, 8), (1, 4))),
        "lengths": ragged_sizes(splits[3], DOCS, PACK_TOKENS, MOST, 2).astype(jnp.int32),
        "out_weight": gaussian(splits[4], (QUERY_HEADS * HEAD_SIZE, D), (QUERY_HEADS * HEAD_SIZE) ** -0.5, 0.09375, ((1, 4),)),
    }


def reference(queries, keys, values, lengths, out_weight):
    token_total_count = queries.shape[0]
    query_group_size = QUERY_HEADS // KEY_VALUE_HEADS
    window = MOST + TOK_DEV
    positions = jnp.arange(token_total_count, dtype=jnp.int32)
    boundary = jnp.cumsum(lengths)
    labels = jnp.sum((boundary[None, :] <= positions[:, None]).astype(jnp.int32), axis=1) + 1
    grouped_queries = queries.reshape(token_total_count, KEY_VALUE_HEADS, query_group_size, HEAD_SIZE)
    keyed_rows = keys.reshape(token_total_count, KEY_VALUE_HEADS, HEAD_SIZE)
    valued_rows = values.reshape(token_total_count, KEY_VALUE_HEADS, HEAD_SIZE)

    def one_block(block_index):
        q_start = (block_index * TOK_DEV).astype(jnp.int32)
        k_start = jnp.clip(q_start - MOST, 0, token_total_count - window).astype(jnp.int32)
        q_part = lax.dynamic_slice_in_dim(grouped_queries, q_start, TOK_DEV, 0).astype(jnp.float32)
        k_part = lax.dynamic_slice_in_dim(keyed_rows, k_start, window, 0).astype(jnp.float32)
        v_part = lax.dynamic_slice_in_dim(valued_rows, k_start, window, 0).astype(jnp.float32)
        q_label = lax.dynamic_slice_in_dim(labels, q_start, TOK_DEV, 0)
        k_label = lax.dynamic_slice_in_dim(labels, k_start, window, 0)
        q_pos = lax.dynamic_slice_in_dim(positions, q_start, TOK_DEV, 0)
        k_pos = lax.dynamic_slice_in_dim(positions, k_start, window, 0)
        scores = jnp.einsum("tkgd,skd->kgts", q_part, k_part) * (HEAD_SIZE ** -0.5)
        allowed = (q_label[:, None] == k_label[None, :]) & (k_pos[None, :] <= q_pos[:, None])
        scores = jnp.where(allowed, scores, -1e30)
        top = jnp.max(scores, axis=-1)
        weights = jnp.exp(scores - top[..., None])
        total = jnp.sum(weights, axis=-1)
        rounded = weights.astype(jnp.bfloat16).astype(jnp.float32)
        numer = jnp.einsum("kgts,skd->kgtd", rounded, v_part)
        attended = numer / total[..., None]
        attended = jnp.transpose(attended, (2, 0, 1, 3)).reshape(TOK_DEV, QUERY_HEADS * HEAD_SIZE)
        return attended.astype(jnp.bfloat16)

    blocks = lax.map(one_block, jnp.arange(token_total_count // TOK_DEV, dtype=jnp.int32))
    attended = blocks.reshape(token_total_count, QUERY_HEADS * HEAD_SIZE)
    return jnp.dot(attended, out_weight, preferred_element_type=jnp.float32).astype(jnp.bfloat16)
```

```python
import functools

import jax
import jax.numpy as jnp
from jax import lax
from jax.experimental import pallas as pl
from jax.experimental.pallas import tpu as pltpu
from jax.sharding import PartitionSpec as P

HEAD_SIZE = 128
LOG2E = 1.4426950408889634
MASKED = -1e30


def shifted(shard, axis, by):
    peers = lax.axis_size(axis)
    pairs = [(i, i + by) for i in range(peers) if 0 <= i + by < peers]
    return lax.ppermute(shard, axis, pairs)


def attention_kernel(
    group, reach, tok, tile, length_ref, q_ref, k_ref, v_ref, *rest
):
    carried = rest[:reach]
    out_ref, kbuf, vbuf, acc, top, total, sems = rest[reach:]
    step = pl.program_id(0)
    documents = length_ref.shape[0]
    heads = q_ref.shape[1] // HEAD_SIZE
    me = lax.axis_index("ctx")
    base = me * tok + step * tile
    scale = HEAD_SIZE ** (-0.5) * LOG2E

    @pl.when(step == 0)
    def _():
        own = pl.ds(group * HEAD_SIZE, HEAD_SIZE)
        copies = [
            pltpu.make_async_copy(k_ref.at[:, own], kbuf.at[pl.ds(reach * tok, tok)], sems.at[0]),
            pltpu.make_async_copy(v_ref.at[:, own], vbuf.at[pl.ds(reach * tok, tok)], sems.at[1]),
        ]
        for s in range(reach):
            rows = pl.ds((reach - 1 - s) * tok, tok)
            copies += [
                pltpu.make_async_copy(
                    carried[s].at[:, pl.ds(0, HEAD_SIZE)], kbuf.at[rows], sems.at[2 * s + 2]
                ),
                pltpu.make_async_copy(
                    carried[s].at[:, pl.ds(HEAD_SIZE, HEAD_SIZE)], vbuf.at[rows], sems.at[2 * s + 3]
                ),
            ]
        for copy in copies:
            copy.start()
        for copy in copies:
            copy.wait()

    pos = base + lax.broadcasted_iota(jnp.int32, (tile, 1), 0)

    def find(d, state):
        edge, begin, first = state
        edge = edge + length_ref[d]
        begin = jnp.where(pos >= edge, edge, begin)
        first = jnp.where(base >= edge, edge, first)
        return edge, begin, first

    zero = jnp.int32(0)
    _, begin, first = lax.fori_loop(
        0, documents, find, (zero, jnp.zeros((tile, 1), jnp.int32), zero)
    )
    window = (me - reach) * tok
    diagonal = reach * (tok // tile) + step
    lowest = lax.div(first - window, jnp.int32(tile))

    def visit(j, initial):
        rows = pl.ds(pl.multiple_of(j * tile, tile), tile)
        k = kbuf[rows, :]
        v = vbuf[rows, :]
        key = window + j * tile + lax.broadcasted_iota(jnp.int32, (tile, tile), 1)
        allowed = key >= begin
        if initial:
            allowed = allowed & (key <= pos)
        for h in range(heads):
            at = pl.ds(h * tile, tile)
            s = lax.dot_general(
                q_ref[:, h * HEAD_SIZE : (h + 1) * HEAD_SIZE],
                k,
                (((1,), (1,)), ((), ())),
                preferred_element_type=jnp.float32,
            )
            s = jnp.where(allowed, s, MASKED)
            high = jnp.max(s, axis=1, keepdims=True)
            if initial:
                p = jnp.exp2((s - high) * scale)
                add = p[:, :HEAD_SIZE]
                for c in range(1, tile // HEAD_SIZE):
                    add = add + p[:, c * HEAD_SIZE : (c + 1) * HEAD_SIZE]
                total[at, :] = add
                top[at, :] = jnp.broadcast_to(high, (tile, HEAD_SIZE))
                acc[at, :] = jnp.dot(
                    p.astype(jnp.bfloat16), v, preferred_element_type=jnp.float32
                )
            else:
                old = top[at, :]
                new = jnp.maximum(old, high)
                factor = jnp.exp2((old - new) * scale)
                p = jnp.exp2((s - new[:, :1]) * scale)
                add = p[:, :HEAD_SIZE]
                for c in range(1, tile // HEAD_SIZE):
                    add = add + p[:, c * HEAD_SIZE : (c + 1) * HEAD_SIZE]
                total[at, :] = total[at, :] * factor + add
                top[at, :] = new
                acc[at, :] = acc[at, :] * factor + jnp.dot(
                    p.astype(jnp.bfloat16), v, preferred_element_type=jnp.float32
                )

    visit(diagonal, True)

    def earlier(j, _):
        visit(j, False)
        return 0

    lax.fori_loop(lowest, diagonal, earlier, 0)
    for h in range(heads):
        at = pl.ds(h * tile, tile)
        whole = jnp.sum(total[at, :], axis=1, keepdims=True)
        out_ref[:, h * HEAD_SIZE : (h + 1) * HEAD_SIZE] = (acc[at, :] / whole).astype(out_ref.dtype)


def attention(lengths, queries, keys, values, carried, group):
    tok, features = queries.shape
    kv_heads = keys.shape[1] // HEAD_SIZE
    wide = features // kv_heads
    heads = wide // HEAD_SIZE
    reach = len(carried)
    tile = min(256, tok)
    span = (reach + 1) * tok
    return pl.pallas_call(
        functools.partial(attention_kernel, group, reach, tok, tile),
        out_shape=jax.ShapeDtypeStruct((tok, wide), queries.dtype),
        grid=(tok // tile,),
        in_specs=[
            pl.BlockSpec(memory_space=pltpu.SMEM),
            pl.BlockSpec((tile, wide), lambda i: (i, group)),
        ]
        + [pl.BlockSpec(memory_space=pl.ANY)] * (2 + reach),
        out_specs=pl.BlockSpec((tile, wide), lambda i: (i, 0)),
        scratch_shapes=[
            pltpu.VMEM((span, HEAD_SIZE), keys.dtype),
            pltpu.VMEM((span, HEAD_SIZE), values.dtype),
            pltpu.VMEM((heads * tile, HEAD_SIZE), jnp.float32),
            pltpu.VMEM((heads * tile, HEAD_SIZE), jnp.float32),
            pltpu.VMEM((heads * tile, HEAD_SIZE), jnp.float32),
            pltpu.SemaphoreType.DMA((2 + 2 * reach,)),
        ],
        compiler_params=pltpu.CompilerParams(vmem_limit_bytes=16 << 20),
        cost_estimate=pl.CostEstimate(
            flops=4 * tok * wide * tok * 2, bytes_accessed=4 * tok * wide, transcendentals=tok * heads * tok * 2
        ),
        name=f"attention_{group}",
    )(lengths, queries, keys, values, *carried)


def project_kernel(count, given, plan_ref, *refs):
    pieces, weights = refs[:count], refs[count : 2 * count]
    out_ref = refs[2 * count + given]
    acc = refs[-1]
    if given:
        acc[...] = refs[2 * count][...]
    else:
        acc[...] = jnp.zeros_like(acc)
    for i in range(count):

        @pl.when(plan_ref[count + i] != 0)
        def _():
            acc[...] += jnp.dot(
                pieces[i][...], weights[i][...], preferred_element_type=jnp.float32
            )

    out_ref[...] = acc[...].astype(out_ref.dtype)


def project(pieces, plan, weight, total, out_dtype):
    tok, deep = pieces[0].shape
    count = len(pieces)
    columns = weight.shape[1]
    tile = min(256, columns)
    given = 0 if total is None else 1
    in_specs = [pl.BlockSpec((tok, deep), lambda n, plan: (0, 0)) for _ in pieces]
    in_specs += [
        pl.BlockSpec((deep, tile), functools.partial(lambda i, n, plan: (plan[i], n), i))
        for i in range(count)
    ]
    if given:
        in_specs.append(pl.BlockSpec((tok, tile), lambda n, plan: (0, n)))
    return pl.pallas_call(
        functools.partial(project_kernel, count, given),
        out_shape=jax.ShapeDtypeStruct((tok, columns), out_dtype),
        grid_spec=pltpu.PrefetchScalarGridSpec(
            num_scalar_prefetch=1,
            grid=(columns // tile,),
            in_specs=in_specs,
            out_specs=pl.BlockSpec((tok, tile), lambda n, plan: (0, n)),
            scratch_shapes=[pltpu.VMEM((tok, tile), jnp.float32)],
        ),
        compiler_params=pltpu.CompilerParams(vmem_limit_bytes=24 << 20),
        cost_estimate=pl.CostEstimate(
            flops=2 * tok * deep * columns * count,
            bytes_accessed=2 * count * deep * (tok + columns) + 8 * tok * columns,
            transcendentals=0,
        ),
        name=f"project_{count}_{given}",
    )(plan, *pieces, *([weight] * count), *([] if total is None else [total]))


def shards(queries, keys, values, lengths, out_weight):
    kv_local = keys.shape[1] // HEAD_SIZE
    planes = lax.axis_size("head")
    plane = lax.axis_index("head")
    reach = lax.axis_size("ctx") // 4

    pieces, attended = [], []
    for g in range(kv_local):
        cols = slice(g * HEAD_SIZE, (g + 1) * HEAD_SIZE)
        both = jnp.concatenate([keys[:, cols], values[:, cols]], axis=1)
        pieces.append([shifted(both, "ctx", s + 1) for s in range(reach)])
    for g in range(kv_local):
        attended.append(attention(lengths, queries, keys, values, pieces[g], g))

    def plan_of(offsets):
        index, valid = [], []
        for off in offsets:
            source = plane + off
            for g in range(kv_local):
                index.append(jnp.clip(source, 0, planes - 1) * kv_local + g)
                valid.append(((source >= 0) & (source < planes)).astype(jnp.int32))
        return jnp.stack(index + valid).astype(jnp.int32)

    total = project(attended, plan_of([0]), out_weight, None, jnp.float32)
    right, left = attended, attended
    for hop in range(1, planes):
        right = [shifted(r, "head", 1) for r in right]
        left = [shifted(l, "head", -1) for l in left]
        last = hop == planes - 1
        total = project(
            right + left,
            plan_of([-hop, hop]),
            out_weight,
            total,
            queries.dtype if last else jnp.float32,
        )
    return total


def solution(mesh):
    return jax.shard_map(
        shards,
        mesh=mesh,
        in_specs=(P("ctx", "head"), P("ctx", "head"), P("ctx", "head"), P(), P(None, "head")),
        out_specs=P("ctx", "head"),
        check_vma=False,
    )
```

```python
import functools

import jax
import jax.numpy as jnp
from jax import lax
from jax.experimental import pallas as pl
from jax.experimental.pallas import tpu as pltpu
from jax.sharding import PartitionSpec as P

HEAD_SIZE = 128
LOG2E = 1.4426950408889634
MASKED = -1e30
SCALE = HEAD_SIZE ** (-0.5) * LOG2E


def shifted(shard, axis, by):
    peers = lax.axis_size(axis)
    pairs = [(i, i + by) for i in range(peers) if 0 <= i + by < peers]
    return lax.ppermute(shard, axis, pairs)


def lanes(x, n):
    return x if n == 1 else jnp.concatenate([x] * n, axis=1)


def score(q, k, allowed):
    s = lax.dot_general(q, k, (((1,), (1,)), ((), ())), preferred_element_type=jnp.float32)
    return jnp.where(allowed, s, MASKED)


def lane_sum(p):
    add = p[:, :HEAD_SIZE]
    for c in range(1, p.shape[1] // HEAD_SIZE):
        add = add + p[:, c * HEAD_SIZE : (c + 1) * HEAD_SIZE]
    return add


def diagonal_kernel(tok, tile, groups, length_ref, q_ref, k_ref, v_ref, begin_ref, *state):
    step = pl.program_id(0)
    documents = length_ref.shape[0]
    heads = q_ref.shape[1] // HEAD_SIZE // groups
    shard = lax.axis_index("ctx") * tok
    base = shard + step * tile
    pos = base + lax.broadcasted_iota(jnp.int32, (tile, HEAD_SIZE), 0)
    edge = jnp.int32(0)
    begin = jnp.zeros((tile, HEAD_SIZE), jnp.int32)
    first = jnp.int32(0)
    for d in range(documents):
        edge = edge + length_ref[d]
        begin = jnp.where(pos >= edge, edge, begin)
        first = jnp.where(base >= edge, edge, first)
    begin_ref[...] = begin
    wide = lanes(begin, tile // HEAD_SIZE)
    row = base + lax.broadcasted_iota(jnp.int32, (tile, tile), 0)
    lowest = lax.div(jnp.maximum(first - shard, 0), jnp.int32(tile))

    def visit(j, initial):
        rows = pl.ds(pl.multiple_of(j * tile, tile), tile)
        key = shard + j * tile + lax.broadcasted_iota(jnp.int32, (tile, tile), 1)
        allowed = key >= wide
        if initial:
            allowed = allowed & (key <= row)
        for g in range(groups):
            k = k_ref[rows, g * HEAD_SIZE : (g + 1) * HEAD_SIZE]
            v = v_ref[rows, g * HEAD_SIZE : (g + 1) * HEAD_SIZE]
            acc, top, total = state[3 * g : 3 * g + 3]
            for h in range(heads):
                at = slice(h * HEAD_SIZE, (h + 1) * HEAD_SIZE)
                full = g * heads + h
                q = q_ref[:, full * HEAD_SIZE : (full + 1) * HEAD_SIZE]
                update(acc, top, total, at, score(q, k, allowed), v, initial)

    visit(step, True)

    def earlier(j, _):
        visit(j, False)
        return 0

    lax.fori_loop(lowest, step, earlier, 0)


def update(acc, top, total, at, s, v, initial):
    high = jnp.max(s, axis=1, keepdims=True)
    copies = s.shape[1] // HEAD_SIZE
    if initial:
        new = jnp.broadcast_to(high, (s.shape[0], HEAD_SIZE))
        p = jnp.exp2((s - lanes(new, copies)) * SCALE)
        total[:, at] = lane_sum(p)
        top[:, at] = new
        acc[:, at] = jnp.dot(p.astype(jnp.bfloat16), v, preferred_element_type=jnp.float32)
    else:
        old = top[:, at]
        new = jnp.maximum(old, high)
        factor = jnp.exp2((old - new) * SCALE)
        p = jnp.exp2((s - lanes(new, copies)) * SCALE)
        total[:, at] = total[:, at] * factor + lane_sum(p)
        top[:, at] = new
        acc[:, at] = acc[:, at] * factor + jnp.dot(
            p.astype(jnp.bfloat16), v, preferred_element_type=jnp.float32
        )


def diagonal(lengths, queries, keys, values):
    tok, features = queries.shape
    groups = keys.shape[1] // HEAD_SIZE
    tile = min(256, tok)
    wide = features // groups
    state = jax.ShapeDtypeStruct((tok, wide), jnp.float32)
    outs = pl.pallas_call(
        functools.partial(diagonal_kernel, tok, tile, groups),
        out_shape=[jax.ShapeDtypeStruct((tok, HEAD_SIZE), jnp.int32)] + [state] * (3 * groups),
        grid=(tok // tile,),
        in_specs=[
            pl.BlockSpec(memory_space=pltpu.SMEM),
            pl.BlockSpec((tile, features), lambda i: (i, 0)),
            pl.BlockSpec(keys.shape, lambda i: (0, 0)),
            pl.BlockSpec(values.shape, lambda i: (0, 0)),
        ],
        out_specs=[pl.BlockSpec((tile, HEAD_SIZE), lambda i: (i, 0))]
        + [pl.BlockSpec((tile, wide), lambda i: (i, 0))] * (3 * groups),
        compiler_params=pltpu.CompilerParams(vmem_limit_bytes=24 << 20),
        cost_estimate=pl.CostEstimate(
            flops=4 * tok * features * tok, bytes_accessed=16 * tok * features, transcendentals=tok * tok
        ),
        name="diagonal",
    )(lengths, queries, keys, values)
    return outs[0], [outs[1 + 3 * g : 4 + 3 * g] for g in range(groups)]


def earlier_kernel(tok, tile, reach, length_ref, q_ref, begin_ref, acc_in, top_in, total_in, *rest):
    carried = rest[:reach]
    out_ref, acc, top, total = rest[reach:]
    step = pl.program_id(0)
    documents = length_ref.shape[0]
    heads = q_ref.shape[1] // HEAD_SIZE
    me = lax.axis_index("ctx")
    base = me * tok + step * tile
    edge = jnp.int32(0)
    first = jnp.int32(0)
    for d in range(documents):
        edge = edge + length_ref[d]
        first = jnp.where(base >= edge, edge, first)
    acc[...] = acc_in[...]
    top[...] = top_in[...]
    total[...] = total_in[...]
    for s in range(reach):
        shard = (me - 1 - s) * tok
        lowest = lax.div(jnp.clip(first - shard, 0, tok), jnp.int32(tile))

        def visit(j, _):
            rows = pl.ds(pl.multiple_of(j * tile, tile), tile)
            k = carried[s][rows, :HEAD_SIZE]
            v = carried[s][rows, HEAD_SIZE:]
            key = shard + j * tile + lax.broadcasted_iota(jnp.int32, (tile, tile), 1)
            allowed = key >= lanes(begin_ref[...], tile // HEAD_SIZE)
            for h in range(heads):
                at = slice(h * HEAD_SIZE, (h + 1) * HEAD_SIZE)
                update(acc, top, total, at, score(q_ref[:, at], k, allowed), v, False)
            return 0

        lax.fori_loop(lowest, tok // tile, visit, 0)
    for h in range(heads):
        at = slice(h * HEAD_SIZE, (h + 1) * HEAD_SIZE)
        whole = jnp.sum(total[:, at], axis=1, keepdims=True)
        out_ref[:, at] = (acc[:, at] / whole).astype(out_ref.dtype)


def earlier(lengths, queries, begin, state, carried, group):
    tok = queries.shape[0]
    wide = state[0].shape[1]
    reach = len(carried)
    tile = min(256, tok)
    block = pl.BlockSpec((tile, wide), lambda i: (i, 0))
    scratch = pltpu.VMEM((tile, wide), jnp.float32)
    return pl.pallas_call(
        functools.partial(earlier_kernel, tok, tile, reach),
        out_shape=jax.ShapeDtypeStruct((tok, wide), queries.dtype),
        grid=(tok // tile,),
        in_specs=[
            pl.BlockSpec(memory_space=pltpu.SMEM),
            pl.BlockSpec((tile, wide), lambda i: (i, group)),
            pl.BlockSpec((tile, HEAD_SIZE), lambda i: (i, 0)),
            block,
            block,
            block,
        ]
        + [pl.BlockSpec(carried[0].shape, lambda i: (0, 0))] * reach,
        out_specs=block,
        scratch_shapes=[scratch] * 3,
        compiler_params=pltpu.CompilerParams(vmem_limit_bytes=24 << 20),
        cost_estimate=pl.CostEstimate(
            flops=4 * tok * wide * tok * reach, bytes_accessed=16 * tok * wide, transcendentals=tok * tok * reach
        ),
        name=f"earlier_{group}",
    )(lengths, queries, begin, *state, *carried)


def pick(table, plane):
    chosen = jnp.int32(-1)
    for z, value in enumerate(table):
        chosen = jnp.where(plane == z, jnp.int32(value), chosen)
    return chosen


def project_kernel(origins, groups, given, weight_ref, *refs):
    count = len(origins)
    pieces = refs[:count]
    out_ref, acc, buf, sems = refs[count + given :]
    deep = pieces[0].shape[1]
    plane = lax.axis_index("head")
    sources = [plane if table is None else pick(table, plane) for table, _ in origins]

    def fetch(i):
        rows = pl.ds(pl.multiple_of((sources[i] * groups + origins[i][1]) * deep, deep), deep)
        return pltpu.make_async_copy(weight_ref.at[rows, :], buf.at[i], sems.at[i])

    for i in range(count):

        @pl.when(sources[i] >= 0)
        def _():
            fetch(i).start()

    acc[...] = refs[count][...] if given else jnp.zeros_like(acc)
    tile = min(256, acc.shape[1])
    for i in range(count):

        @pl.when(sources[i] >= 0)
        def _():
            fetch(i).wait()
            for n in range(acc.shape[1] // tile):
                cols = slice(n * tile, (n + 1) * tile)
                acc[:, cols] += jnp.dot(
                    pieces[i][...], buf[i, :, cols], preferred_element_type=jnp.float32
                )

    out_ref[...] = acc[...].astype(out_ref.dtype)


def project(pieces, origins, groups, weight, total, out_dtype):
    tok, deep = pieces[0].shape
    count = len(pieces)
    columns = weight.shape[1]
    given = 0 if total is None else 1
    whole = pl.BlockSpec(memory_space=pltpu.VMEM)
    return pl.pallas_call(
        functools.partial(project_kernel, origins, groups, given),
        out_shape=jax.ShapeDtypeStruct((tok, columns), out_dtype),
        in_specs=[pl.BlockSpec(memory_space=pltpu.HBM)] + [whole] * (count + given),
        out_specs=whole,
        scratch_shapes=[
            pltpu.VMEM((tok, columns), jnp.float32),
            pltpu.VMEM((count, deep, columns), weight.dtype),
            pltpu.SemaphoreType.DMA((count,)),
        ],
        compiler_params=pltpu.CompilerParams(vmem_limit_bytes=28 << 20),
        cost_estimate=pl.CostEstimate(
            flops=2 * tok * deep * columns * count,
            bytes_accessed=2 * count * deep * (tok + columns) + 8 * tok * columns,
            transcendentals=0,
        ),
        name=f"project_{count}_{given}",
    )(weight, *pieces, *([] if total is None else [total]))


def train(planes, start):
    hold = list(range(planes))
    hops = []
    parity = start
    while True:
        pairs, later = [], [-1] * planes
        for z in range(planes):
            peer = z + 1 if z % 2 == parity else z - 1
            if 0 <= peer < planes and hold[z] >= 0:
                pairs.append((z, peer))
                later[peer] = hold[z]
        if not pairs:
            return hops
        hops.append((pairs, later))
        hold, parity = later, 1 - parity


def shards(queries, keys, values, lengths, out_weight):
    groups = keys.shape[1] // HEAD_SIZE
    planes = lax.axis_size("head")
    plane = lax.axis_index("head")
    reach = lax.axis_size("ctx") // 4

    def bundle(g):
        cols = slice(g * HEAD_SIZE, (g + 1) * HEAD_SIZE)
        return jnp.concatenate([keys[:, cols], values[:, cols]], axis=1)

    trains = [train(planes, 0), train(planes, 1)]
    hops = max(len(t) for t in trains)

    def advance(hop, held):
        return [
            lax.ppermute(p, "head", t[hop][0]) if hop < len(t) else None
            for t, p in zip(trains, held)
        ]

    carried = [[shifted(bundle(0), "ctx", s + 1) for s in range(reach)]]
    begin, state = diagonal(lengths, queries, keys, values)
    own, held = [], []
    for g in range(groups):
        if g + 1 < groups:
            after, carried[g], begin = lax.optimization_barrier((bundle(g + 1), carried[g], begin))
            carried.append([shifted(after, "ctx", s + 1) for s in range(reach)])
        own.append(earlier(lengths, queries, begin, state[g], carried[g], g))
        held.append(advance(0, [own[g], own[g]]))

    total = None
    pieces, origins = list(own), [(None, g) for g in range(groups)]
    for hop in range(1, hops + 1):
        for g in range(groups):
            here = held[g]
            if hop < hops:
                if total is not None:
                    here, total = lax.optimization_barrier((here, total))
                held[g] = advance(hop, here)
            for t, p in zip(trains, here):
                if p is not None:
                    pieces.append(p)
                    origins.append((t[hop - 1][1], g))
            last = hop == hops and g == groups - 1
            total = project(
                pieces, origins, groups, out_weight, total, queries.dtype if last else jnp.float32
            )
            pieces, origins = [], []
    return total


def solution(mesh):
    return jax.shard_map(
        shards,
        mesh=mesh,
        in_specs=(P("ctx", "head"), P("ctx", "head"), P("ctx", "head"), P(), P(None, "head")),
        out_specs=P("ctx", "head"),
        check_vma=False,
    )
```

```python
import functools

import jax
import jax.numpy as jnp
from jax import lax
from jax.experimental import pallas as pl
from jax.experimental.pallas import tpu as pltpu
from jax.sharding import PartitionSpec as P

HEAD_SIZE = 128
LOG2E = 1.4426950408889634
MASKED = -1e30
SCALE = HEAD_SIZE ** (-0.5) * LOG2E


def shifted(shard, axis, by):
    peers = lax.axis_size(axis)
    pairs = [(i, i + by) for i in range(peers) if 0 <= i + by < peers]
    return lax.ppermute(shard, axis, pairs)


def lanes(x, n):
    return x if n == 1 else jnp.concatenate([x] * n, axis=1)


def score(q, k, allowed):
    s = lax.dot_general(q, k, (((1,), (1,)), ((), ())), preferred_element_type=jnp.float32)
    return jnp.where(allowed, s, MASKED)


def lane_sum(p):
    add = p[:, :HEAD_SIZE]
    for c in range(1, p.shape[1] // HEAD_SIZE):
        add = add + p[:, c * HEAD_SIZE : (c + 1) * HEAD_SIZE]
    return add


def fetch_all(copies):
    for copy in copies:
        copy.start()
    for copy in copies:
        copy.wait()


def diagonal_kernel(at, only_ends, length_ref, q_any, k_any, v_any, acc_out, top_out, total_out, *rest):
    begin_ref, qbuf, kbuf, vbuf, acc, top, total, sems = rest
    tok, wide = qbuf.shape
    tile = acc.shape[0]
    documents = length_ref.shape[0]
    sources = [(q_any, qbuf, wide), (k_any, kbuf, HEAD_SIZE), (v_any, vbuf, HEAD_SIZE)]
    shard = lax.axis_index("ctx") * tok

    def run():
        fetch_all(
            [
                pltpu.make_async_copy(src.at[:, pl.ds(at[i], width)], dst, sems.at[i])
                for i, (src, dst, width) in enumerate(sources)
            ]
        )

        def one(step, _):
            mine = pl.ds(pl.multiple_of(step * tile, tile), tile)
            base = shard + step * tile
            pos = base + lax.broadcasted_iota(jnp.int32, (tile, HEAD_SIZE), 0)
            edge = jnp.int32(0)
            begin = jnp.zeros((tile, HEAD_SIZE), jnp.int32)
            first = jnp.int32(0)
            for d in range(documents):
                edge = edge + length_ref[d]
                begin = jnp.where(pos >= edge, edge, begin)
                first = jnp.where(base >= edge, edge, first)
            begin_ref[mine, :] = begin
            row = base + lax.broadcasted_iota(jnp.int32, (tile, tile), 0)
            lowest = lax.div(jnp.maximum(first - shard, 0), jnp.int32(tile))

            def visit(j, initial):
                rows = pl.ds(pl.multiple_of(j * tile, tile), tile)
                key = shard + j * tile + lax.broadcasted_iota(jnp.int32, (tile, tile), 1)
                allowed = key >= lanes(begin_ref[mine, :], tile // HEAD_SIZE)
                if initial:
                    allowed = allowed & (key <= row)
                for h in range(wide // HEAD_SIZE):
                    cols = slice(h * HEAD_SIZE, (h + 1) * HEAD_SIZE)
                    s = score(qbuf[mine, cols], kbuf[rows, :], allowed)
                    update(acc, top, total, cols, s, vbuf[rows, :], initial)

            visit(step, True)

            def before(j, _):
                visit(j, False)
                return 0

            lax.fori_loop(lowest, step, before, 0)
            acc_out[mine, :] = acc[...]
            top_out[mine, :] = top[...]
            total_out[mine, :] = total[...]
            return 0

        lax.fori_loop(0, tok // tile, one, 0)

    guarded(only_ends, run)


def guarded(only_ends, run):
    if only_ends:
        plane = lax.axis_index("head")
        pl.when((plane == 0) | (plane == lax.axis_size("head") - 1))(run)
    else:
        run()


def update(acc, top, total, at, s, v, initial):
    high = jnp.max(s, axis=1, keepdims=True)
    copies = s.shape[1] // HEAD_SIZE
    if initial:
        new = jnp.broadcast_to(high, (s.shape[0], HEAD_SIZE))
        p = jnp.exp2((s - lanes(new, copies)) * SCALE)
        total[:, at] = lane_sum(p)
        top[:, at] = new
        acc[:, at] = jnp.dot(p.astype(jnp.bfloat16), v, preferred_element_type=jnp.float32)
    else:
        old = top[:, at]
        new = jnp.maximum(old, high)
        factor = jnp.exp2((old - new) * SCALE)
        p = jnp.exp2((s - lanes(new, copies)) * SCALE)
        total[:, at] = total[:, at] * factor + lane_sum(p)
        top[:, at] = new
        acc[:, at] = acc[:, at] * factor + jnp.dot(
            p.astype(jnp.bfloat16), v, preferred_element_type=jnp.float32
        )


def diagonal(lengths, arrays, at, wide, only_ends):
    tok = arrays[0].shape[0]
    tile = min(256, tok)
    state = jax.ShapeDtypeStruct((tok, wide), jnp.float32)
    whole = pl.BlockSpec(memory_space=pltpu.VMEM)
    hbm = pl.BlockSpec(memory_space=pltpu.HBM)
    dtype = arrays[0].dtype
    return pl.pallas_call(
        functools.partial(diagonal_kernel, at, only_ends),
        out_shape=[state] * 3 + [jax.ShapeDtypeStruct((tok, HEAD_SIZE), jnp.int32)],
        in_specs=[pl.BlockSpec(memory_space=pltpu.SMEM), hbm, hbm, hbm],
        out_specs=[whole] * 4,
        scratch_shapes=[
            pltpu.VMEM((tok, wide), dtype),
            pltpu.VMEM((tok, HEAD_SIZE), dtype),
            pltpu.VMEM((tok, HEAD_SIZE), dtype),
        ]
        + [pltpu.VMEM((tile, wide), jnp.float32)] * 3
        + [pltpu.SemaphoreType.DMA((3,))],
        compiler_params=pltpu.CompilerParams(vmem_limit_bytes=16 << 20),
        cost_estimate=pl.CostEstimate(
            flops=4 * tok * wide * tok, bytes_accessed=16 * tok * wide, transcendentals=tok * tok
        ),
        name="diagonal_ends" if only_ends else "diagonal",
    )(lengths, *arrays)


def earlier_kernel(at, only_ends, reach, length_ref, q_any, acc_in, top_in, total_in, begin_ref, *rest):
    carried = rest[:reach]
    out_ref, qbuf, acc, top, total, sem = rest[reach:]
    tok, wide = qbuf.shape
    tile = acc.shape[0]
    documents = length_ref.shape[0]
    me = lax.axis_index("ctx")

    def run():
        fetch_all([pltpu.make_async_copy(q_any.at[:, pl.ds(at, wide)], qbuf, sem)])

        def one(step, _):
            mine = pl.ds(pl.multiple_of(step * tile, tile), tile)
            base = me * tok + step * tile
            edge = jnp.int32(0)
            first = jnp.int32(0)
            for d in range(documents):
                edge = edge + length_ref[d]
                first = jnp.where(base >= edge, edge, first)
            acc[...] = acc_in[mine, :]
            top[...] = top_in[mine, :]
            total[...] = total_in[mine, :]
            for s in range(reach):
                shard = (me - 1 - s) * tok
                lowest = lax.div(jnp.clip(first - shard, 0, tok), jnp.int32(tile))

                def visit(j, _):
                    rows = pl.ds(pl.multiple_of(j * tile, tile), tile)
                    k = carried[s][rows, :HEAD_SIZE]
                    v = carried[s][rows, HEAD_SIZE:]
                    key = shard + j * tile + lax.broadcasted_iota(jnp.int32, (tile, tile), 1)
                    allowed = key >= lanes(begin_ref[mine, :], tile // HEAD_SIZE)
                    for h in range(wide // HEAD_SIZE):
                        cols = slice(h * HEAD_SIZE, (h + 1) * HEAD_SIZE)
                        scores = score(qbuf[mine, cols], k, allowed)
                        update(acc, top, total, cols, scores, v, False)
                    return 0

                lax.fori_loop(lowest, tok // tile, visit, 0)
            for h in range(wide // HEAD_SIZE):
                cols = slice(h * HEAD_SIZE, (h + 1) * HEAD_SIZE)
                whole = jnp.sum(total[:, cols], axis=1, keepdims=True)
                out_ref[mine, cols] = (acc[:, cols] / whole).astype(out_ref.dtype)
            return 0

        lax.fori_loop(0, tok // tile, one, 0)

    guarded(only_ends, run)


def earlier(lengths, queries, at, state, carried, only_ends):
    tok, wide = state[0].shape
    reach = len(carried)
    tile = min(256, tok)
    whole = pl.BlockSpec(memory_space=pltpu.VMEM)
    return pl.pallas_call(
        functools.partial(earlier_kernel, at, only_ends, reach),
        out_shape=jax.ShapeDtypeStruct((tok, wide), queries.dtype),
        in_specs=[pl.BlockSpec(memory_space=pltpu.SMEM), pl.BlockSpec(memory_space=pltpu.HBM)]
        + [whole] * (4 + reach),
        out_specs=whole,
        scratch_shapes=[pltpu.VMEM((tok, wide), queries.dtype)]
        + [pltpu.VMEM((tile, wide), jnp.float32)] * 3
        + [pltpu.SemaphoreType.DMA],
        compiler_params=pltpu.CompilerParams(vmem_limit_bytes=16 << 20),
        cost_estimate=pl.CostEstimate(
            flops=4 * tok * wide * tok * reach, bytes_accessed=16 * tok * wide, transcendentals=tok * tok * reach
        ),
        name="earlier_ends" if only_ends else "earlier",
    )(lengths, queries, *state, *carried)


def pick(table, plane):
    chosen = jnp.int32(-1)
    for z, value in enumerate(table):
        chosen = jnp.where(plane == z, jnp.int32(value), chosen)
    return chosen


def project_kernel(origins, groups, given, weight_ref, *refs):
    count = len(origins)
    pieces = refs[:count]
    out_ref, acc, buf, sems = refs[count + given :]
    deep = pieces[0].shape[1]
    plane = lax.axis_index("head")
    sources = [plane if table is None else pick(table, plane) for table, _ in origins]

    def fetch(i):
        rows = pl.ds(pl.multiple_of((sources[i] * groups + origins[i][1]) * deep, deep), deep)
        return pltpu.make_async_copy(weight_ref.at[rows, :], buf.at[i], sems.at[i])

    for i in range(count):

        @pl.when(sources[i] >= 0)
        def _():
            fetch(i).start()

    acc[...] = refs[count][...] if given else jnp.zeros_like(acc)
    tile = min(256, acc.shape[1])
    for i in range(count):

        @pl.when(sources[i] >= 0)
        def _():
            fetch(i).wait()
            for n in range(acc.shape[1] // tile):
                cols = slice(n * tile, (n + 1) * tile)
                acc[:, cols] += jnp.dot(
                    pieces[i][...], buf[i, :, cols], preferred_element_type=jnp.float32
                )

    out_ref[...] = acc[...].astype(out_ref.dtype)


def project(pieces, origins, groups, weight, total, out_dtype):
    tok, deep = pieces[0].shape
    count = len(pieces)
    columns = weight.shape[1]
    given = 0 if total is None else 1
    whole = pl.BlockSpec(memory_space=pltpu.VMEM)
    return pl.pallas_call(
        functools.partial(project_kernel, origins, groups, given),
        out_shape=jax.ShapeDtypeStruct((tok, columns), out_dtype),
        in_specs=[pl.BlockSpec(memory_space=pltpu.HBM)] + [whole] * (count + given),
        out_specs=whole,
        scratch_shapes=[
            pltpu.VMEM((tok, columns), jnp.float32),
            pltpu.VMEM((count, deep, columns), weight.dtype),
            pltpu.SemaphoreType.DMA((count,)),
        ],
        compiler_params=pltpu.CompilerParams(vmem_limit_bytes=28 << 20),
        cost_estimate=pl.CostEstimate(
            flops=2 * tok * deep * columns * count,
            bytes_accessed=2 * count * deep * (tok + columns) + 8 * tok * columns,
            transcendentals=0,
        ),
        name=f"project_{count}_{given}",
    )(weight, *pieces, *([] if total is None else [total]))


def train(planes, start, skip):
    hold = list(range(planes))
    hops = []
    parity = start
    while True:
        pairs, later = [], [-1] * planes
        for z in range(planes):
            peer = z + 1 if z % 2 == parity else z - 1
            if 0 <= peer < planes and hold[z] >= 0 and (hops or (z, peer) not in skip):
                pairs.append((z, peer))
                later[peer] = hold[z]
        if not pairs:
            return hops
        hops.append((pairs, later))
        hold, parity = later, 1 - parity


def tied(first, then):
    return lax.optimization_barrier((first, then))


def shards(queries, keys, values, lengths, out_weight):
    groups = keys.shape[1] // HEAD_SIZE
    wide = queries.shape[1] // groups
    planes, parts = lax.axis_size("head"), lax.axis_size("ctx")
    reach = parts // 4
    ends = sorted({0, planes - 1})
    extra = groups - 1
    moves = [(1, 0), (planes - 2, planes - 1)] if planes > 1 else []

    def columns(array, g, width):
        return array[:, g * width : (g + 1) * width]

    def bundle(g):
        return jnp.concatenate([columns(keys, g, HEAD_SIZE), columns(values, g, HEAD_SIZE)], axis=1)

    def trains_of(g):
        skip = moves if g == extra else []
        return [train(planes, 0, skip), train(planes, 1, skip)]

    def advance(hop, g, held):
        return [
            lax.ppermute(p, "head", t[hop][0]) if hop < len(t) else None
            for t, p in zip(trains_of(g), held)
        ]

    def own_diagonal(g):
        at = (g * wide, g * HEAD_SIZE, g * HEAD_SIZE)
        return diagonal(lengths, (queries, keys, values), at, wide, False)

    carried = [[shifted(bundle(0), "ctx", s + 1) for s in range(reach)]]
    moved = jnp.concatenate([columns(queries, extra, wide), bundle(extra)], axis=1)
    moved = lax.ppermute(moved, "head", moves)
    own, held = [], []
    for g in range(groups):
        state = own_diagonal(g)
        if g + 1 < groups:
            state, after = tied(state, bundle(g + 1))
            carried.append([shifted(after, "ctx", s + 1) for s in range(reach)])
        own.append(earlier(lengths, queries, g * wide, state, carried[g], False))
        held.append(advance(0, g, [own[g], own[g]]))

    own[-1], moved = tied(own[-1], moved)
    across = [
        (c * planes + z, (c + s + 1) * planes + z)
        for s in range(reach)
        for c in range(parts - s - 1)
        for z in ends
    ]
    fetched = [
        lax.ppermute(
            moved[:, wide:],
            ("ctx", "head"),
            [(a, b) for a, b in across if b - a == (s + 1) * planes],
        )
        for s in range(reach)
    ]

    hops = max(len(t) for g in range(groups) for t in trains_of(g))
    total = None
    pieces, origins = list(own), [(None, g) for g in range(groups)]
    for hop in range(1, hops + 1):
        for g in range(groups):
            here = held[g]
            if hop < hops:
                if total is not None:
                    total, here = tied(total, here)
                held[g] = advance(hop, g, here)
            for t, p in zip(trains_of(g), here):
                if p is not None:
                    pieces.append(p)
                    origins.append((t[hop - 1][1], g))
            last = hop == hops and g == groups - 1
            total = project(
                pieces, origins, groups, out_weight, total, queries.dtype if last else jnp.float32
            )
            pieces, origins = [], []
            if hop == 1 and g == groups - 1:
                total, moved = tied(total, moved)
                state = diagonal(lengths, (moved,) * 3, (0, wide, wide + HEAD_SIZE), wide, True)
                pieces = [earlier(lengths, moved, 0, state, fetched, True)]
                table = [-1] * planes
                for a, b in moves:
                    table[b] = a
                origins = [(table, extra)]
    return total


def solution(mesh):
    return jax.shard_map(
        shards,
        mesh=mesh,
        in_specs=(P("ctx", "head"), P("ctx", "head"), P("ctx", "head"), P(), P(None, "head")),
        out_specs=P("ctx", "head"),
        check_vma=False,
    )
```
